256 devices in a mesh: tm: 8 (over z_lo, core), height: 32 (over z_hi, y, x).
Axes of the slice: x: 4, y: 4, z: 8 (z_hi: 2, z_lo: 4; z = z_hi * 4 + z_lo), core: 2. Of those that a mesh axis runs over, the one named last changes fastest.
Arguments:
- queries: bfloat16 [32, 32, 32, 2560], P('tm', 'height'), may hold values from -8 to 8
- keys: bfloat16 [32, 32, 32, 2560], P('tm', 'height'), may hold values from -8 to 8
- values: bfloat16 [32, 32, 32, 2560], P('tm', 'height'), may hold values from -6 to 6
- window_mask: int32 [32, 32, 4, 27], P('tm', 'height'), may hold values from 0 to 1, as said below
- pos_t: int32 [32], P('tm'), may hold values from 0 to 511, as said below
- pos_h: int32 [32], P('height'), may hold values from 0 to 63, as said below
- pos_w: int32 [32], replicated, may hold values from 0 to 63, as said below
Outputs:
- attended: bfloat16 [32, 32, 32, 2560], P('tm', 'height')
The draws below stay inside these ranges and needn't reach their ends.
Inputs may be any that keep to these rules, and one draw needn't show every extreme that they name: `window_mask`: entry (dt+1)*9 + (dr+1)*3 + (db+1) refers to the tile offset by dt frames, dr rows and db tiles along the row; it is 0 wherever that tile lies outside the grid, and the centre entry 13 is always 1. `pos_t`: strictly increasing. `pos_h`: strictly increasing. `pos_w`: strictly increasing.
All inputs are finite; a program needn't handle non-finite values.
Results may differ from the reference program's by a relative error of at most 0.0044.
The reference program's roundings to bfloat16 on the way count: a program that leaves them out, or rounds other values in their place, can miss the bound.
Values may be sent and summed in bfloat16 or wider, within the bound.
No kernel may reach another device: no remote copies, remote signals or barrier semaphores. Data moves between devices by JAX's collectives and lax.ppermute only.
A program may use at most 128 MiB of HBM per device.

```python
import math
import jax
import jax.numpy as jnp
from jax import lax

HEADS = 20
HEAD_DIM = 128
C = 2560
W = 32
TILE_W = 8
T_SIZE = 32
H = 32


def query_key_pair(key):
    base = jax.random.fold_in(key, 101)
    streams = jax.random.split(base, 2)
    full_shape = (T_SIZE, H, W, C)
    query_vals = 2.5 * jax.random.normal(streams[0], full_shape, jnp.float32)
    key_vals = jax.random.normal(streams[1], full_shape, jnp.float32)
    return (jnp.clip(query_vals, -8.0, 8.0), jnp.clip(key_vals, -8.0, 8.0))


def draw_queries(key, part):
    return query_key_pair(key)[0].astype(jnp.bfloat16)


def draw_keys(key, part):
    return query_key_pair(key)[1].astype(jnp.bfloat16)


def draw_window_mask(key, part):
    blocks = W // TILE_W
    frame_idx = jnp.arange(T_SIZE).reshape(T_SIZE, 1, 1, 1)
    row_idx = jnp.arange(H).reshape(1, H, 1, 1)
    block_idx = jnp.arange(blocks).reshape(1, 1, blocks, 1)
    offset = jnp.arange(27).reshape(1, 1, 1, 27)
    step_t = offset // 9 - 1
    step_h = offset // 3 % 3 - 1
    step_w = offset % 3 - 1
    inside = (frame_idx + step_t >= 0) & (frame_idx + step_t < T_SIZE) & (row_idx + step_h >= 0) & (row_idx + step_h < H) & (block_idx + step_w >= 0) & (block_idx + step_w < blocks)
    drawn = jax.random.randint(jax.random.fold_in(key, 7), (T_SIZE, H, blocks, 27), 0, 8)
    kept = drawn < 2 + 5 * frame_idx // T_SIZE
    return jnp.where(offset == 13, 1, jnp.where(kept & inside, 1, 0)).astype(jnp.int32)


def ordered_positions(key, length, salt):
    index_all = jnp.arange(length)
    extra = jax.random.randint(jax.random.fold_in(key, salt), (length,), 0, 2)
    positions = 2 * index_all + extra
    positions = jnp.where(index_all == 0, 0, jnp.where(index_all == length - 1, 2 * length - 1, positions))
    return positions.astype(jnp.int32)


def draw_pos_t(key, part):
    index_all = jnp.arange(T_SIZE)
    extra = jax.random.randint(jax.random.fold_in(key, 11), (T_SIZE,), 0, 16)
    return (16 * index_all + extra).astype(jnp.int32)


def draw_pos_h(key, part):
    return ordered_positions(key, H, 13)


def draw_pos_w(key, part):
    return ordered_positions(key, W, 17)


def block_levels(rng, extent, cuts, smallest, largest):
    def one(axis_at, parts):
        draws = jax.random.uniform(jax.random.fold_in(jax.random.fold_in(rng, 6), axis_at), (parts,), jnp.float32, smallest / len(cuts), largest / len(cuts))
        return jnp.repeat(jnp.exp(draws), extent[axis_at] // parts).reshape((-1,) + (1,) * (len(extent) - axis_at - 1))

    level = one(*cuts[0])
    for cut in cuts[1:]:
        level = level * one(*cut)
    return level


def scatter_about(key, dims, width, most, cuts=(), held_as=jnp.bfloat16):
    values = jax.random.normal(key, dims, jnp.float32) * width
    if len(cuts) > 0:
        values = block_levels(key, dims, cuts, -0.22, 0.18) * values
    return jnp.clip(values, min=-most, max=most).astype(held_as)


def setup_inputs(seed: int = 0) -> dict:
    key_of = jax.random.split(jax.random.key(seed), 8)
    return {
        "queries": draw_queries(jax.random.fold_in(key_of[7], 71), 0),
        "keys": draw_keys(jax.random.fold_in(key_of[7], 71), 0),
        "values": scatter_about(key_of[2], (T_SIZE, H, W, C), 1.0, 6.0, ((0, 8), (1, 32))),
        "window_mask": draw_window_mask(jax.random.fold_in(key_of[7], 71), 0),
        "pos_t": draw_pos_t(jax.random.fold_in(key_of[7], 71), 0),
        "pos_h": draw_pos_h(jax.random.fold_in(key_of[7], 71), 0),
        "pos_w": draw_pos_w(jax.random.fold_in(key_of[7], 71), 0),
    }


def rope_tables(pos_t, pos_h, pos_w, half_dim):
    pairs_hw = 2 * half_dim // 6
    pairs_time = half_dim - 2 * pairs_hw
    pair_index = jnp.arange(half_dim).astype(jnp.float32)
    freq_time = jnp.where(pair_index < pairs_time, jnp.power(10000.0, -pair_index / pairs_time), 0.0)
    in_rows = (pair_index >= pairs_time) & (pair_index < pairs_time + pairs_hw)
    freq_rows = jnp.where(in_rows, jnp.power(10000.0, -(pair_index - pairs_time) / pairs_hw), 0.0)
    freq_cols = jnp.where(pair_index >= pairs_time + pairs_hw, jnp.power(10000.0, -(pair_index - pairs_time - pairs_hw) / pairs_hw), 0.0)
    angles = pos_t.astype(jnp.float32)[:, None, None, None] * freq_time + pos_h.astype(jnp.float32)[None, :, None, None] * freq_rows + pos_w.astype(jnp.float32)[None, None, :, None] * freq_cols
    cos_tab = jnp.cos(angles)
    sine_tab = jnp.sin(angles)
    return (jnp.concatenate([cos_tab, cos_tab], -1), jnp.concatenate([-sine_tab, sine_tab], -1))

def rotate(tensor, cos_tab, sine_tab, head_count, head_dim):
    shaped = tensor.astype(jnp.float32).reshape(tensor.shape[:-1] + (head_count, head_dim))
    turned = shaped * cos_tab[..., None, :] + jnp.roll(shaped, head_dim // 2, axis=-1) * sine_tab[..., None, :]
    return turned.reshape(tensor.shape).astype(jnp.bfloat16)

def reference(queries, keys, values, window_mask, pos_t, pos_h, pos_w):
    head_count = HEADS
    head_dim = HEAD_DIM
    tile_len = TILE_W
    blocks = W // tile_len
    score_scale = 1.0 / math.sqrt(head_dim)
    cos_tab, sine_tab = rope_tables(pos_t, pos_h, pos_w, head_dim // 2)
    frame_list = jnp.arange(T_SIZE)

    def rotate_keys(frame_idx):
        return rotate(keys[frame_idx], cos_tab[frame_idx], sine_tab[frame_idx], head_count, head_dim)
    k_rot = lax.map(rotate_keys, frame_list)
    first_k = k_rot[0].reshape(H * W, head_count, head_dim).astype(jnp.float32)
    first_v = values[0].reshape(H * W, head_count, head_dim).astype(jnp.float32)
    padding = ((1, 1), (1, 1), (tile_len, tile_len), (0, 0))
    k_pad = jnp.pad(k_rot, padding)
    v_pad = jnp.pad(values, padding)

    def frame_out(frame_idx):
        q_rot = rotate(queries[frame_idx], cos_tab[frame_idx], sine_tab[frame_idx], head_count, head_dim)
        k_near = lax.dynamic_slice_in_dim(k_pad, frame_idx, 3, 0).reshape(3, H + 2, blocks + 2, tile_len, C)
        v_near = lax.dynamic_slice_in_dim(v_pad, frame_idx, 3, 0).reshape(3, H + 2, blocks + 2, tile_len, C)
        k_win = jnp.stack([k_near[step_t, step_h:step_h + H, step_w:step_w + blocks] for step_t in range(3) for step_h in range(3) for step_w in range(3)], axis=2)
        v_win = jnp.stack([v_near[step_t, step_h:step_h + H, step_w:step_w + blocks] for step_t in range(3) for step_h in range(3) for step_w in range(3)], axis=2)
        k_win = k_win.reshape(H, blocks, 27 * tile_len, head_count, head_dim).astype(jnp.float32)
        v_win = v_win.reshape(H, blocks, 27 * tile_len, head_count, head_dim).astype(jnp.float32)
        q_tiles = q_rot.reshape(H, blocks, tile_len, head_count, head_dim).astype(jnp.float32)
        s_near = jnp.einsum('abqhd,abkhd->abhqk', q_tiles, k_win) * score_scale
        allowed = jnp.repeat(window_mask[frame_idx] > 0, tile_len, axis=2)[:, :, None, None, :]
        q_flat = q_rot.reshape(H * W, head_count, head_dim).astype(jnp.float32)
        s_far = jnp.einsum('nhd,khd->hnk', q_flat, first_k) * score_scale
        s_far = s_far.reshape(head_count, H, blocks, tile_len, H * W).transpose(1, 2, 0, 3, 4)
        row_top = jnp.maximum(jnp.where(allowed, s_near, -1e+30).max(-1), s_far.max(-1))
        p_near = jnp.where(allowed, jnp.exp(s_near - row_top[..., None]), 0.0).astype(jnp.bfloat16)
        p_far = jnp.exp(s_far - row_top[..., None]).astype(jnp.bfloat16)
        row_total = p_near.astype(jnp.float32).sum(-1) + p_far.astype(jnp.float32).sum(-1)
        weighted = jnp.einsum('abhqk,abkhd->abqhd', p_near.astype(jnp.float32), v_win)
        weighted = weighted + jnp.einsum('abhqk,khd->abqhd', p_far.astype(jnp.float32), first_v)
        result = weighted / row_total.transpose(0, 1, 3, 2)[..., None]
        return result.reshape(H, W, C).astype(jnp.bfloat16)
    return lax.map(frame_out, frame_list)
```

```python
import functools
import math

import jax
import jax.numpy as jnp
import numpy as np
from jax import lax
from jax.experimental import pallas as pl
from jax.experimental.pallas import tpu as pltpu
from jax.sharding import PartitionSpec as P

HEADS = 20
D = 128
GROUPS = 4
GH = HEADS // GROUPS
GC = GH * D
TILE = 8
NEG = -1e30
SCALE = 1.0 / math.sqrt(D)
LOG2E = math.log2(math.e)
BF = jnp.bfloat16
F32 = jnp.float32


def freq_row():
    half = D // 2
    n_hw = 2 * half // 6
    n_t = half - 2 * n_hw
    j = np.arange(half)
    e = np.where(j < n_t, j / n_t, np.where(j < n_t + n_hw, (j - n_t) / n_hw, (j - n_t - n_hw) / n_hw))
    f = np.power(10000.0, -e).astype(np.float32)
    return np.concatenate([f, f])[None, :], n_t, n_hw


def tables(pos_t_ref, pos_h_ref, pos_w, freq, frames, width):
    _, n_t, n_hw = freq_row()
    lane = lax.broadcasted_iota(jnp.int32, (width, D), 1) % (D // 2)
    hpos = pos_h_ref[0].astype(F32)
    wpos = jnp.broadcast_to(pos_w, (width, D))
    rows_cos, rows_sin = [], []
    for f in range(frames):
        tpos = pos_t_ref[f].astype(F32)
        pos = jnp.where(lane < n_t, tpos, jnp.where(lane < n_t + n_hw, hpos, wpos))
        ang = pos * freq
        rows_cos.append(jnp.cos(ang))
        s = jnp.sin(ang)
        first = lax.broadcasted_iota(jnp.int32, (width, D), 1) < D // 2
        rows_sin.append(jnp.where(first, -s, s))
    return rows_cos, rows_sin


def turn(x, c, s):
    x = x.astype(F32)
    return (x * c + pltpu.roll(x, D // 2, 1) * s).astype(BF)


def kv_kernel(xi, pos_t, pos_h, pos_w, freq, k, v, o0, o1, o2, o3, far, cos_o, sin_o):
    frames, _, width, _ = k.shape
    cs, sn = tables(pos_t, pos_h, pos_w[...], freq[...], frames, width)
    for f in range(frames):
        cos_o[f] = cs[f]
        sin_o[f] = sn[f]
    for s, o in enumerate((o0, o1, o2, o3)):
        base = lax.rem(xi[0] + s, GROUPS) * GC
        for f in range(frames):
            for h in range(GH):
                at = pl.ds(pl.multiple_of(base + h * D, D), D)
                r = turn(k[f, 0, :, at], cs[f], sn[f])
                o[0, f, :, h * D:(h + 1) * D] = r
                if f == 0:
                    far[s, 0, :, h * D:(h + 1) * D] = r
            val = v[f, 0, :, pl.ds(pl.multiple_of(base, D), GC)]
            o[1, f] = val
            if f == 0:
                far[s, 1] = val


def q_kernel(xi, cos_i, sin_i, q, o0, o1, o2, o3):
    frames, _, width, _ = q.shape
    for s, o in enumerate((o0, o1, o2, o3)):
        base = lax.rem(xi[0] + s, GROUPS) * GC
        for f in range(frames):
            for h in range(GH):
                at = pl.ds(pl.multiple_of(base + h * D, D), D)
                o[f, :, h * D:(h + 1) * D] = turn(q[f, 0, :, at], cos_i[f], sin_i[f])


def bias_kernel(m0, m1, m2, m3, out):
    keys = out.shape[-1]
    width = out.shape[2]
    rows = m0.shape[0] * TILE
    kk = lax.broadcasted_iota(jnp.int32, (D, keys), 1)
    o = lax.broadcasted_iota(jnp.int32, (D, keys), 0)
    g = lax.shift_right_logical(kk, 5)
    dr = (g >= 3).astype(jnp.int32) + (g >= 6).astype(jnp.int32)
    dt = g - 3 * dr
    code = dt * 9 + dr * 3
    k2 = lax.broadcasted_iota(jnp.int32, (rows, keys), 1)
    r2 = lax.broadcasted_iota(jnp.int32, (rows, keys), 0)
    kb = lax.shift_right_logical(k2 & 31, 3)
    b = lax.shift_right_logical(r2 & 31, 3)
    step = kb - b + 1
    for s, m in enumerate((m0, m1, m2, m3)):
        w = m[...].astype(F32)
        wide = jnp.broadcast_to(w[:, None, :], (w.shape[0], TILE, D)).reshape(rows, D).astype(BF)
        ok = jnp.zeros((rows, keys), F32)
        for db in range(3):
            sel = jnp.where(o == code + db, 1.0, 0.0).astype(BF)
            a = jnp.dot(wide, sel, preferred_element_type=F32)
            ok = ok + jnp.where(step == db, a, 0.0)
        out[s] = jnp.where(ok > 0.5, 0.0, NEG).reshape(rows // width, width, keys)


def near_kernel(xi, kv0, kv1, kv2, kv3, hm, hp, tm, tp, cmm, cmp_, cpm, cpp,
                q0, q1, q2, q3, bias, acc, mo, lo, ks, vs):
    x = xi[0]
    frames = kv0.shape[1]
    width = kv0.shape[2]
    rows = GROUPS
    for s, kv in enumerate((kv0, kv1, kv2, kv3)):
        j = lax.rem(x - s + GROUPS, GROUPS) + 1
        for i, dst in enumerate((ks, vs)):
            dst[j, 1:frames + 1] = kv[i]
            dst[j, 0] = tm[s, i]
            dst[j, frames + 1] = tp[s, i]
    for i, dst in enumerate((ks, vs)):
        dst[0, 1:frames + 1] = hm[i]
        dst[rows + 1, 1:frames + 1] = hp[i]
        dst[0, 0] = cmm[i]
        dst[rows + 1, 0] = cmp_[i]
        dst[0, frames + 1] = cpm[i]
        dst[rows + 1, frames + 1] = cpp[i]
    keys = 9 * width
    lane = lax.broadcasted_iota(jnp.int32, (width, D), 1)
    for s, q in enumerate((q0, q1, q2, q3)):
        j = lax.rem(x - s + GROUPS, GROUPS)

        def step(f, c, s=s, q=q, j=j):
            b = bias[s, f]
            tops = jnp.zeros((width, D), F32)
            sums = jnp.zeros((width, D), F32)
            for h in range(GH):
                hs = slice(h * D, (h + 1) * D)
                key = ks[pl.ds(j, 3), pl.ds(f, 3), :, hs].reshape(keys, D)
                val = vs[pl.ds(j, 3), pl.ds(f, 3), :, hs].reshape(keys, D)
                sc = lax.dot_general(q[f, :, hs], key, (((1,), (1,)), ((), ())),
                                     preferred_element_type=F32) + b
                top = jnp.max(sc, axis=-1, keepdims=True)
                p = jnp.exp2((sc - top) * (SCALE * LOG2E)).astype(BF)
                tot = jnp.sum(p.astype(F32), axis=-1, keepdims=True)
                acc[s, f, :, hs] = jnp.dot(p, val, preferred_element_type=F32)
                tops = jnp.where(lane == h, top, tops)
                sums = jnp.where(lane == h, tot, sums)
            mo[s, f] = tops
            lo[s, f] = sums
            return c

        lax.fori_loop(0, frames, step, 0)


def far_kernel(q0, q1, q2, q3, acc, mi, li, *rest):
    fars = rest[:8]
    outs = rest[8:12]
    frames, width = q0.shape[:2]
    n = frames * width
    for h in range(GH):
        hs = slice(h * D, (h + 1) * D)
        key = jnp.concatenate([f[:, 0, :, hs].reshape(-1, D) for f in fars], axis=0)
        val = jnp.concatenate([f[:, 1, :, hs].reshape(-1, D) for f in fars], axis=0)
        for s, (q, o) in enumerate(zip((q0, q1, q2, q3), outs)):
            qq = q[:, :, hs].reshape(n, D)
            sc = lax.dot_general(qq, key, (((1,), (1,)), ((), ())), preferred_element_type=F32)
            mn = mi[s, :, :, h:h + 1].reshape(n, 1)
            ln = li[s, :, :, h:h + 1].reshape(n, 1)
            top = jnp.maximum(mn, jnp.max(sc, axis=-1, keepdims=True))
            p = jnp.exp2((sc - top) * (SCALE * LOG2E)).astype(BF)
            fix = jnp.exp2((mn - top) * (SCALE * LOG2E))
            tot = ln * fix + jnp.sum(p.astype(F32), axis=-1, keepdims=True)
            num = acc[s, :, :, hs].reshape(n, D) * fix + jnp.dot(p, val, preferred_element_type=F32)
            o[:, :, hs] = (num / tot).astype(BF).reshape(frames, width, D)


def join_kernel(xi, r0, r1, r2, r3, out):
    for s, r in enumerate((r0, r1, r2, r3)):
        base = lax.rem(xi[0] + s, GROUPS) * GC
        out[:, 0, :, pl.ds(pl.multiple_of(base, D), GC)] = r[...]


def call(kernel, args, outs, smem=0, scratch=(), flops=1000000):
    specs = [pl.BlockSpec(memory_space=pltpu.SMEM)] * smem
    specs += [pl.BlockSpec(memory_space=pltpu.VMEM)] * (len(args) - smem)
    many = isinstance(outs, (list, tuple))
    ospec = [pl.BlockSpec(memory_space=pltpu.VMEM) for _ in outs] if many else pl.BlockSpec(memory_space=pltpu.VMEM)
    size = sum(a.size * a.dtype.itemsize for a in args)
    return pl.pallas_call(
        kernel,
        out_shape=outs,
        in_specs=specs,
        out_specs=ospec,
        scratch_shapes=list(scratch),
        cost_estimate=pl.CostEstimate(flops=flops, bytes_accessed=size, transcendentals=0),
        compiler_params=pltpu.CompilerParams(vmem_limit_bytes=48 * 1024 * 1024),
    )(*args)


def xshift(s):
    return [(i, i // 4 * 4 + (i + s) % 4) for i in range(32)]


def yshift(s):
    return [(i, i // 16 * 16 + ((i // 4 + s) % 4) * 4 + i % 4) for i in range(32)]


def rowshift(s):
    return [(i, i + s) for i in range(32) if 0 <= i + s < 32]


def tmshift(s):
    return [(i, i + s) for i in range(8) if 0 <= i + s < 8]


def diag(dt, dr):
    return [(t * 32 + r, (t + dt) * 32 + r + dr) for t in range(8) for r in range(32)
            if 0 <= t + dt < 8 and 0 <= r + dr < 32]


def per_device(queries, keys, values, window_mask, pos_t, pos_h, pos_w):
    frames, _, width, _ = queries.shape
    ti = lax.axis_index("tm")
    hi = lax.axis_index("height")
    x = hi % 4
    xi = x.reshape(1).astype(jnp.int32)
    both = ("tm", "height")
    sds = jax.ShapeDtypeStruct
    freq = jnp.asarray(freq_row()[0])
    wcol = pos_w.astype(F32).reshape(width, 1)

    kvs = [sds((2, frames, width, GC), BF)] * 4
    tab = sds((frames, width, D), F32)
    *kv, far, cos_t, sin_t = call(
        kv_kernel, (xi, pos_t, pos_h, wcol, freq, keys, values),
        kvs + [sds((4, 2, width, GC), BF), tab, tab], smem=3)

    kvr = [kv[0]] + [lax.ppermute(kv[s], "height", xshift(s)) for s in (1, 2, 3)]

    low = [lax.ppermute(far, "tm", [(0, 2 * k)]) for k in (1, 2, 3)]
    mine = jnp.where(ti == 0, far, low[0] + low[1] + low[2])
    other = lax.ppermute(mine, both, [(t * 32 + r, (t + 1) * 32 + (r + 16) % 32)
                                      for t in range(0, 8, 2) for r in range(32)])
    mine = jnp.where(ti % 2 == 0, mine, other)

    q = call(q_kernel, (xi, cos_t, sin_t, queries), [sds((frames, width, GC), BF)] * 4, smem=1)

    small = jnp.pad(window_mask.reshape(frames * 4, 27).astype(BF), ((0, 0), (0, D - 27)))
    masks = [small] + [lax.ppermute(small, "height", xshift(s)) for s in (1, 2, 3)]
    bias = call(bias_kernel, tuple(masks), sds((4, frames, width, 9 * width), F32))

    def row_of(j):
        at = (x - j) % 4
        return jnp.where(at < 2, jnp.where(at == 0, kvr[0], kvr[1]), jnp.where(at == 2, kvr[2], kvr[3]))

    first, last = row_of(0), row_of(3)
    hm = lax.ppermute(last, "height", rowshift(4))
    hp = lax.ppermute(first, "height", rowshift(-4))
    ends = frames - 1
    tm = lax.ppermute(jnp.stack([a[:, ends] for a in kvr]), "tm", tmshift(1))
    tp = lax.ppermute(jnp.stack([a[:, 0] for a in kvr]), "tm", tmshift(-1))
    cmm = lax.ppermute(last[:, ends], both, diag(1, 4))
    cmp_ = lax.ppermute(first[:, ends], both, diag(1, -4))
    cpm = lax.ppermute(last[:, 0], both, diag(-1, 4))
    cpp = lax.ppermute(first[:, 0], both, diag(-1, -4))

    qr = [q[0]] + [lax.ppermute(q[s], "height", xshift(s)) for s in (1, 2, 3)]

    xf = [mine[0]] + [lax.ppermute(mine[s], "height", xshift(s)) for s in (1, 2, 3)]
    unit = jnp.stack(xf)
    units = [unit] + [lax.ppermute(unit, "height", yshift(s)) for s in (1, 3, 2)]
    swap = [(i, i ^ 1) for i in range(8)]
    units = units + [lax.ppermute(u, "tm", swap) for u in units]

    ext = pltpu.VMEM((GROUPS + 2, frames + 2, width, GC), BF)
    acc, mo, lo = call(
        near_kernel, (xi, *kvr, hm, hp, tm, tp, cmm, cmp_, cpm, cpp, *qr, bias),
        [sds((4, frames, width, GC), F32), sds((4, frames, width, D), F32), sds((4, frames, width, D), F32)],
        smem=1, scratch=(ext, ext))
    outs = call(far_kernel, (*qr, acc, mo, lo, *units), [sds((frames, width, GC), BF)] * 4)
    back = [outs[0]] + [lax.ppermute(outs[s], "height", xshift(-s)) for s in (1, 2, 3)]
    return call(join_kernel, (xi, *back), sds((frames, 1, width, HEADS * D), BF), smem=1)


def solution(mesh):
    wide = P("tm", "height", None, None)
    return jax.shard_map(
        per_device,
        mesh=mesh,
        in_specs=(wide, wide, wide, wide, P("tm"), P("height"), P()),
        out_specs=wide,
        check_vma=False,
    )
```

```python
import functools
import math

import jax
import jax.numpy as jnp
from jax import lax
from jax.experimental import pallas as pl
from jax.experimental.pallas import tpu as pltpu
from jax.sharding import PartitionSpec as P


HEADS = 20
D = 128
GROUPS = 4
GH = HEADS // GROUPS
GC = GH * D
TILE = 8
NEG = -1e30
SCALE = 1.0 / math.sqrt(D)
LOG2E = math.log2(math.e)
BF = jnp.bfloat16
F32 = jnp.float32


def half_split():
    half = D // 2
    n_hw = 2 * half // 6
    return half - 2 * n_hw, n_hw


def tables(pos_t, pos_h, pos_w, frames, width):
    n_t, n_hw = half_split()
    row = lax.broadcasted_iota(jnp.int32, (width, D), 0)
    full = lax.broadcasted_iota(jnp.int32, (width, D), 1)
    lane = full & (D // 2 - 1)
    j = lane.astype(F32)
    power = jnp.where(lane < n_t, j / n_t, jnp.where(lane < n_t + n_hw, (j - n_t) / n_hw, (j - n_t - n_hw) / n_hw))
    freq = jnp.exp(power * (-math.log(10000.0)))
    hpos = pos_h[0].astype(F32)
    wpos = jnp.zeros((width, D), F32)
    for i in range(width):
        wpos = jnp.where(row == i, pos_w[i].astype(F32), wpos)
    fixed = jnp.where(lane < n_t + n_hw, hpos, wpos)
    rows_cos, rows_sin = [], []
    for f in range(frames):
        ang = jnp.where(lane < n_t, pos_t[f].astype(F32), fixed) * freq
        rows_cos.append(jnp.cos(ang))
        s = jnp.sin(ang)
        rows_sin.append(jnp.where(full < D // 2, -s, s))
    return rows_cos, rows_sin


def turn(x, c, s):
    x = x.astype(F32)
    return (x * c + pltpu.roll(x, D // 2, 1) * s).astype(BF)


def kv_kernel(xi, hbuf, pos_t, pos_w, k, v, o0, o1, o2, o3, far, cos_o, sin_o,
              tbuf, wbuf, kbuf, vbuf, small_sem, k_sem, v_sem):
    frames, width = kbuf.shape[:2]
    tiny = [pltpu.make_async_copy(src, dst, small_sem.at[i])
            for i, (src, dst) in enumerate(((pos_t, tbuf), (pos_w, wbuf)))]
    for c in tiny:
        c.start()
    kc = [pltpu.make_async_copy(k.at[f, 0], kbuf.at[f], k_sem.at[f]) for f in range(frames)]
    vc = [pltpu.make_async_copy(v.at[f, 0], vbuf.at[f], v_sem.at[f]) for f in range(frames)]
    for f in range(frames):
        kc[f].start()
    for f in range(frames):
        vc[f].start()
    for c in tiny:
        c.wait()
    cs, sn = tables(tbuf, hbuf, wbuf, frames, width)
    outs = (o0, o1, o2, o3)
    base = [lax.rem(xi[0] + s, GROUPS) * GC for s in range(GROUPS)]
    for f in range(frames):
        cos_o[f] = cs[f]
        sin_o[f] = sn[f]
        kc[f].wait()
        for s, o in enumerate(outs):
            for h in range(GH):
                at = pl.ds(pl.multiple_of(base[s] + h * D, D), D)
                r = turn(kbuf[f, :, at], cs[f], sn[f])
                o[f, 0, :, h * D:(h + 1) * D] = r
                if f == 0:
                    far[s, 0, :, h * D:(h + 1) * D] = r
    for f in range(frames):
        vc[f].wait()
        for s, o in enumerate(outs):
            val = vbuf[f, :, pl.ds(pl.multiple_of(base[s], D), GC)]
            o[f, 1] = val
            if f == 0:
                far[s, 1] = val


def q_kernel(xi, cos_i, sin_i, q, o0, o1, o2, o3):
    frames, _, _, _ = q.shape
    for s, o in enumerate((o0, o1, o2, o3)):
        base = lax.rem(xi[0] + s, GROUPS) * GC
        for f in range(frames):
            for h in range(GH):
                at = pl.ds(pl.multiple_of(base + h * D, D), D)
                o[f, :, h * D:(h + 1) * D] = turn(q[f, 0, :, at], cos_i[f], sin_i[f])


def bias_kernel(m0, m1, m2, m3, inner, outer):
    n = inner.shape[1]
    frames = m0.shape[0] // 4
    lane = lax.broadcasted_iota(jnp.int32, (frames * 4, D), 1)
    row = lax.broadcasted_iota(jnp.int32, (frames * 4, D), 0)
    place = lane - 16 * lax.shift_right_logical(row, 2) - (row & 3)

    def picker(keys, where_is):
        kk = lax.broadcasted_iota(jnp.int32, (D, keys), 1)
        o = lax.broadcasted_iota(jnp.int32, (D, keys), 0)
        ft, dr = where_is(lax.shift_right_logical(kk, 5))
        kb = lax.shift_right_logical(kk & 31, 3)
        return jnp.where(o == ft * 16 + dr * 5 + kb + 1, 1.0, 0.0).astype(BF)

    def inner_at(g):
        dr = (g >= frames).astype(jnp.int32) + (g >= 2 * frames).astype(jnp.int32)
        return g - frames * dr + 1, dr

    def outer_at(g):
        late = (g >= 3).astype(jnp.int32)
        return late * (frames + 1), g - 3 * late

    picks = [(inner, picker(inner.shape[2], inner_at)), (outer, picker(outer.shape[2], outer_at))]
    for s, m in enumerate((m0, m1, m2, m3)):
        w = m[...].astype(F32)
        at = jnp.zeros((frames * 4, D), F32)
        for i in range(27):
            at = at + jnp.where(place == i // 9 * 16 + i // 3 % 3 * 5 + i % 3, w[:, i:i + 1], 0.0)
        wide = jnp.broadcast_to(at[:, None, :], (frames * 4, TILE, D)).reshape(n, D).astype(BF)
        for out, sel in picks:
            ok = jnp.dot(wide, sel, preferred_element_type=F32)
            out[s] = jnp.where(ok > 0.5, 0.0, NEG)


def ext_row(x, s):
    return lax.rem(x - s + GROUPS, GROUPS) + 1 if s < GROUPS else (s - GROUPS) * (GROUPS + 1)


def edge_kernel(xi, *refs):
    up, down = refs[-2:]
    for s, r in enumerate(refs[:-2]):
        up[ext_row(xi[0], s)] = r[r.shape[0] - 1]
        down[ext_row(xi[0], s)] = r[0]


def scores(q, key):
    return lax.dot_general(q, key, (((1,), (1,)), ((), ())), preferred_element_type=F32)


def weigh(sc, top):
    return jnp.exp2((sc - top) * (SCALE * LOG2E))


def highest(sc):
    return jnp.max(sc, axis=-1, keepdims=True)


def ones_beside(val):
    return jnp.concatenate([val, jnp.ones_like(val)], axis=1)


def mix(p, val):
    return jnp.dot(p, val, preferred_element_type=F32)


def near_kernel(xi, kv0, kv1, kv2, kv3, hm, hp, u0, u1,
                q0, q1, q2, q3, bias, acc, mo, lo, ks, vs):
    x = xi[0]
    frames = kv0.shape[0]
    width = kv0.shape[2]
    n = frames * width
    for s, kv in enumerate((kv0, kv1, kv2, kv3, hm, hp)):
        for i, dst in enumerate((ks, vs)):
            dst[ext_row(x, s)] = kv[:, i]
    keys = 3 * frames * width
    lane = lax.broadcasted_iota(jnp.int32, (n, D), 1)
    tops = [jnp.zeros((n, D), F32)] * GROUPS
    sums = [jnp.zeros((n, D), F32)] * GROUPS
    for h in range(GH):
        hs = slice(h * D, (h + 1) * D)
        fkey = jnp.concatenate([f[:, 0, :, hs].reshape(-1, D) for f in (u0, u1)], axis=0)
        fval = ones_beside(jnp.concatenate([f[:, 1, :, hs].reshape(-1, D) for f in (u0, u1)], axis=0))
        for s, q in enumerate((q0, q1, q2, q3)):
            j = lax.rem(x - s + GROUPS, GROUPS)
            key = ks[pl.ds(j, 3), :, :, hs].reshape(keys, D)
            val = ones_beside(vs[pl.ds(j, 3), :, :, hs].reshape(keys, D))
            qq = q[:, :, hs].reshape(n, D)
            sc = scores(qq, key) + bias[s]
            sf = scores(qq, fkey)
            top = jnp.maximum(highest(sc), highest(sf))
            p = weigh(sc, top).astype(BF)
            pf = weigh(sf, top).astype(BF)
            r = mix(p, val) + mix(pf, fval)
            acc[s, :, hs] = r[:, :D]
            tops[s] = jnp.where(lane == h, top, tops[s])
            sums[s] = jnp.where(lane == h, r[:, D:], sums[s])
    for s in range(GROUPS):
        mo[s] = tops[s]
        lo[s] = sums[s]


def far_kernel(s, xi, q, acc, mi, li, tm, tp, bias, *refs):
    fars, out = refs[:-1], refs[-1]
    frames, width = q.shape[:2]
    n = frames * width
    j = lax.rem(xi[0] - s + GROUPS, GROUPS)
    for h in range(GH):
        hs = slice(h * D, (h + 1) * D)
        key = jnp.concatenate([f[:, 0, :, hs].reshape(-1, D) for f in fars], axis=0)
        val = ones_beside(jnp.concatenate([f[:, 1, :, hs].reshape(-1, D) for f in fars], axis=0))
        ekey = jnp.concatenate([t[pl.ds(j, 3), 0, :, hs].reshape(-1, D) for t in (tm, tp)], axis=0)
        evl = ones_beside(jnp.concatenate([t[pl.ds(j, 3), 1, :, hs].reshape(-1, D) for t in (tm, tp)], axis=0))
        qq = q[:, :, hs].reshape(n, D)
        sc = scores(qq, key)
        se = scores(qq, ekey) + bias[s]
        mn = mi[s, :, h:h + 1]
        top = jnp.maximum(mn, jnp.maximum(highest(sc), highest(se)))
        p = weigh(sc, top).astype(BF)
        pe = weigh(se, top).astype(BF)
        fix = weigh(mn, top)
        r = mix(p, val) + mix(pe, evl)
        tot = li[s, :, h:h + 1] * fix + r[:, D:]
        num = acc[s, :, hs] * fix + r[:, :D]
        out[:, :, hs] = (num / tot).astype(BF).reshape(frames, width, D)


def join_kernel(xi, r0, r1, r2, r3, out):
    for s, r in enumerate((r0, r1, r2, r3)):
        base = lax.rem(xi[0] + s, GROUPS) * GC
        out[:, 0, :, pl.ds(pl.multiple_of(base, D), GC)] = r[...]


def call(kernel, args, outs, smem=0, hbm=0, scratch=(), flops=1000000):
    specs = [pl.BlockSpec(memory_space=pltpu.SMEM)] * smem
    specs += [pl.BlockSpec(memory_space=pltpu.HBM)] * hbm
    specs += [pl.BlockSpec(memory_space=pltpu.VMEM)] * (len(args) - smem - hbm)
    many = isinstance(outs, (list, tuple))
    ospec = [pl.BlockSpec(memory_space=pltpu.VMEM) for _ in outs] if many else pl.BlockSpec(memory_space=pltpu.VMEM)
    size = sum(a.size * a.dtype.itemsize for a in args)
    return pl.pallas_call(
        kernel,
        out_shape=outs,
        in_specs=specs,
        out_specs=ospec,
        scratch_shapes=list(scratch),
        cost_estimate=pl.CostEstimate(flops=flops, bytes_accessed=size, transcendentals=0),
        compiler_params=pltpu.CompilerParams(vmem_limit_bytes=48 * 1024 * 1024),
    )(*args)


def xshift(s):
    return [(i, i // 4 * 4 + (i + s) % 4) for i in range(32)]


def yshift(s):
    return [(i, i // 16 * 16 + ((i // 4 + s) % 4) * 4 + i % 4) for i in range(32)]


def rowshift(s):
    return [(i, i + s) for i in range(32) if 0 <= i + s < 32]


def tmshift(s):
    return [(i, i + s) for i in range(8) if 0 <= i + s < 8]


def per_device(queries, keys, values, window_mask, pos_t, pos_h, pos_w):
    frames, _, width, _ = queries.shape
    ti = lax.axis_index("tm")
    hi = lax.axis_index("height")
    x = hi % 4
    xi = x.reshape(1).astype(jnp.int32)
    both = ("tm", "height")
    sds = jax.ShapeDtypeStruct
    n = frames * width

    kvs = [sds((frames, 2, width, GC), BF)] * 4
    tab = sds((frames, width, D), F32)
    dma = pltpu.SemaphoreType.DMA
    *kv, far, cos_t, sin_t = call(
        kv_kernel, (xi, pos_h, *[pltpu.with_memory_space_constraint(a, pltpu.HBM) for a in (pos_t, pos_w, keys, values)]),
        kvs + [sds((4, 2, width, GC), BF), tab, tab], smem=2, hbm=4,
        scratch=(pltpu.SMEM((frames,), jnp.int32), pltpu.SMEM((width,), jnp.int32),
                 pltpu.VMEM((frames, width, HEADS * D), BF), pltpu.VMEM((frames, width, HEADS * D), BF),
                 dma((2,)), dma((frames,)), dma((frames,))))

    kvr = [kv[0]] + [lax.ppermute(kv[s], "height", xshift(s)) for s in (1, 2, 3)]

    twin = lax.ppermute(far, "tm", [(0, 1)])
    seed = jnp.where(ti == 1, twin, far)
    near = lambda k: [(r, 2 * k * 32 + r) for r in range(32)] if k < 4 else []
    cross = lambda k: [(32 + r, (2 * k + 1) * 32 + (r + 16) % 32) for r in range(32)]
    spread = [lax.ppermute(seed, both, near(3 - k) + cross(k)) if k < 3 else lax.ppermute(seed, both, cross(3))
              for k in range(4)]
    mine = jnp.where(ti == 0, far, (spread[0] + spread[1]) + (spread[2] + spread[3]))

    q = call(q_kernel, (xi, cos_t, sin_t, queries), [sds((frames, width, GC), BF)] * 4, smem=1)

    small = jnp.pad(window_mask.reshape(frames * 4, 27).astype(BF), ((0, 0), (0, D - 27)))
    masks = [small] + [lax.ppermute(small, "height", xshift(s)) for s in (1, 2, 3)]
    inner, outer = call(bias_kernel, tuple(masks),
                        [sds((4, n, 3 * frames * width), F32), sds((4, n, 6 * width), F32)])

    def row_of(j):
        at = (x - j) % 4
        return jnp.where(at < 2, jnp.where(at == 0, kvr[0], kvr[1]), jnp.where(at == 2, kvr[2], kvr[3]))

    first, last = row_of(0), row_of(3)
    hm = lax.ppermute(last, "height", rowshift(4))
    hp = lax.ppermute(first, "height", rowshift(-4))
    rows = kvr + [hm, hp]
    edge = sds((len(rows), 2, width, GC), BF)
    up, down = call(edge_kernel, (xi, *rows), [edge, edge], smem=1)
    tm = lax.ppermute(up, "tm", tmshift(1))
    tp = lax.ppermute(down, "tm", tmshift(-1))

    qr = [q[0]] + [lax.ppermute(q[s], "height", xshift(s)) for s in (1, 2, 3)]

    xf = [mine[0]] + [lax.ppermute(mine[s], "height", xshift(s)) for s in (1, 2, 3)]
    unit = jnp.stack(xf)
    units = [unit] + [lax.ppermute(unit, "height", yshift(s)) for s in (1, 3, 2)]
    swap = [(i, i ^ 1) for i in range(8)]
    units = units + [lax.ppermute(u, "tm", swap) for u in units]

    ext = pltpu.VMEM((GROUPS + 2, frames, width, GC), BF)
    acc, mo, lo = call(
        near_kernel, (xi, *kvr, hm, hp, units[0], units[4], *qr, inner),
        [sds((4, n, GC), F32), sds((4, n, D), F32), sds((4, n, D), F32)],
        smem=1, scratch=(ext, ext))
    back = [None] * 4
    rest = units[1:4] + units[5:8]
    for s in (2, 1, 3, 0):
        o = call(functools.partial(far_kernel, s), (xi, qr[s], acc, mo, lo, tm, tp, outer, *rest),
                 sds((frames, width, GC), BF), smem=1)
        back[s] = lax.ppermute(o, "height", xshift(-s)) if s else o
    return call(join_kernel, (xi, *back), sds((frames, 1, width, HEADS * D), BF), smem=1)


def solution(mesh):
    wide = P("tm", "height", None, None)

    return jax.shard_map(
        per_device,
        mesh=mesh,
        in_specs=(wide, wide, wide, wide, P("tm"), P("height"), P()),
        out_specs=wide,
        check_vma=False,
    )
```

```python
import functools
import math

import jax
import jax.numpy as jnp
from jax import lax
from jax.experimental import pallas as pl
from jax.experimental.pallas import tpu as pltpu
from jax.sharding import PartitionSpec as P


HEADS = 20
D = 128
GROUPS = 4
GH = HEADS // GROUPS
GC = GH * D
TILE = 8
NEG = -1e30
SCALE = 1.0 / math.sqrt(D)
LOG2E = math.log2(math.e)
BF = jnp.bfloat16
F32 = jnp.float32


def half_split():
    half = D // 2
    n_hw = 2 * half // 6
    return half - 2 * n_hw, n_hw


def tables(pos_t, pos_h, pos_w, frames, width):
    n_t, n_hw = half_split()
    row = lax.broadcasted_iota(jnp.int32, (width, D), 0)
    full = lax.broadcasted_iota(jnp.int32, (width, D), 1)
    lane = full & (D // 2 - 1)
    j = lane.astype(F32)
    power = jnp.where(lane < n_t, j / n_t, jnp.where(lane < n_t + n_hw, (j - n_t) / n_hw, (j - n_t - n_hw) / n_hw))
    freq = jnp.exp(power * (-math.log(10000.0)))
    hpos = pos_h[0].astype(F32)
    wpos = jnp.zeros((width, D), F32)
    for i in range(width):
        wpos = jnp.where(row == i, pos_w[i].astype(F32), wpos)
    fixed = jnp.where(lane < n_t + n_hw, hpos, wpos)
    rows_cos, rows_sin = [], []
    for f in range(frames):
        ang = jnp.where(lane < n_t, pos_t[f].astype(F32), fixed) * freq
        rows_cos.append(jnp.cos(ang))
        s = jnp.sin(ang)
        rows_sin.append(jnp.where(full < D // 2, -s, s))
    return rows_cos, rows_sin


def turn(x, c, s):
    x = x.astype(F32)
    return (x * c + pltpu.roll(x, D // 2, 1) * s).astype(BF)


def kv_kernel(xi, hbuf, pos_t, pos_w, k, v, o0, o1, o2, o3, far, cos_o, sin_o,
              tbuf, wbuf, kbuf, vbuf, small_sem, k_sem, v_sem):
    frames, width = kbuf.shape[:2]
    tiny = [pltpu.make_async_copy(src, dst, small_sem.at[i])
            for i, (src, dst) in enumerate(((pos_t, tbuf), (pos_w, wbuf)))]
    for c in tiny:
        c.start()
    kc = [pltpu.make_async_copy(k.at[f, 0], kbuf.at[f], k_sem.at[f]) for f in range(frames)]
    vc = [pltpu.make_async_copy(v.at[f, 0], vbuf.at[f], v_sem.at[f]) for f in range(frames)]
    for f in range(frames):
        kc[f].start()
    for f in range(frames):
        vc[f].start()
    for c in tiny:
        c.wait()
    cs, sn = tables(tbuf, hbuf, wbuf, frames, width)
    outs = (o0, o1, o2, o3)
    base = [lax.rem(xi[0] + s, GROUPS) * GC for s in range(GROUPS)]
    for f in range(frames):
        cos_o[f] = cs[f]
        sin_o[f] = sn[f]
        kc[f].wait()
        for s, o in enumerate(outs):
            for h in range(GH):
                at = pl.ds(pl.multiple_of(base[s] + h * D, D), D)
                r = turn(kbuf[f, :, at], cs[f], sn[f])
                o[f, 0, :, h * D:(h + 1) * D] = r
                if f == 0:
                    far[s, 0, :, h * D:(h + 1) * D] = r
    for f in range(frames):
        vc[f].wait()
        for s, o in enumerate(outs):
            val = vbuf[f, :, pl.ds(pl.multiple_of(base[s], D), GC)]
            o[f, 1] = val
            if f == 0:
                far[s, 1] = val


def q_kernel(xi, cos_i, sin_i, q, o0, o1, o2, o3):
    frames, _, _, _ = q.shape
    for s, o in enumerate((o0, o1, o2, o3)):
        base = lax.rem(xi[0] + s, GROUPS) * GC
        for f in range(frames):
            for h in range(GH):
                at = pl.ds(pl.multiple_of(base + h * D, D), D)
                o[f, :, h * D:(h + 1) * D] = turn(q[f, 0, :, at], cos_i[f], sin_i[f])


def bias_kernel(fi, m0, m1, m2, m3, inner, outer):
    n = inner.shape[1]
    frames = m0.shape[0] // 4
    lane = lax.broadcasted_iota(jnp.int32, (frames * 4, D), 1)
    row = lax.broadcasted_iota(jnp.int32, (frames * 4, D), 0)
    place = lane - 16 * lax.shift_right_logical(row, 2) - (row & 3)

    def picker(keys, where_is):
        kk = lax.broadcasted_iota(jnp.int32, (D, keys), 1)
        o = lax.broadcasted_iota(jnp.int32, (D, keys), 0)
        ft, dr = where_is(lax.shift_right_logical(kk, 5))
        kb = lax.shift_right_logical(kk & 31, 3)
        return jnp.where(o == ft * 16 + dr * 5 + kb + 1, 1.0, 0.0).astype(BF)

    def inner_at(g):
        dr = (g >= frames).astype(jnp.int32) + (g >= 2 * frames).astype(jnp.int32)
        return g - frames * dr + 1, dr

    def outer_at(g):
        late = (g >= 3).astype(jnp.int32)
        after = jnp.where(fi[0] == 0, 1 - late, late)
        return after * (frames + 1), g - 3 * late

    picks = [(inner, picker(inner.shape[2], inner_at)), (outer, picker(outer.shape[2], outer_at))]
    for s, m in enumerate((m0, m1, m2, m3)):
        w = m[...].astype(F32)
        at = jnp.zeros((frames * 4, D), F32)
        for i in range(27):
            at = at + jnp.where(place == i // 9 * 16 + i // 3 % 3 * 5 + i % 3, w[:, i:i + 1], 0.0)
        wide = jnp.broadcast_to(at[:, None, :], (frames * 4, TILE, D)).reshape(n, D).astype(BF)
        for out, sel in picks:
            ok = jnp.dot(wide, sel, preferred_element_type=F32)
            out[s] = jnp.where(ok > 0.5, 0.0, NEG)


def ext_row(xi, ri, s):
    if s < GROUPS:
        return lax.rem(xi[0] - s + GROUPS, GROUPS) + 1
    low = ri[0] if s == GROUPS else 1 - ri[0]
    return (1 - low) * (GROUPS + 1)


def edge_kernel(xi, ri, fi, *refs):
    inside, across = refs[-2:]
    for s, r in enumerate(refs[:-2]):
        ends = r.shape[0] - 1
        inside[ext_row(xi, ri, s)] = r[(1 - fi[0]) * ends]
        across[ext_row(xi, ri, s)] = r[fi[0] * ends]


def scores(q, key):
    return lax.dot_general(q, key, (((1,), (1,)), ((), ())), preferred_element_type=F32)


def weigh(sc, top):
    return jnp.exp2((sc - top) * (SCALE * LOG2E))


def highest(sc):
    return jnp.max(sc, axis=-1, keepdims=True)


def ones_beside(val):
    return jnp.concatenate([val, jnp.ones_like(val)], axis=1)


def mix(p, val):
    return jnp.dot(p, val, preferred_element_type=F32)


def near_kernel(xi, ri, kv0, kv1, kv2, kv3, h1, h2, u0, u1,
                q0, q1, q2, q3, bias, acc, mo, lo, ks, vs):
    x = xi[0]
    frames = kv0.shape[0]
    width = kv0.shape[2]
    n = frames * width
    for s, kv in enumerate((kv0, kv1, kv2, kv3, h1, h2)):
        for i, dst in enumerate((ks, vs)):
            dst[ext_row(xi, ri, s)] = kv[:, i]
    keys = 3 * frames * width
    lane = lax.broadcasted_iota(jnp.int32, (n, D), 1)
    tops = [jnp.zeros((n, D), F32)] * GROUPS
    sums = [jnp.zeros((n, D), F32)] * GROUPS
    for h in range(GH):
        hs = slice(h * D, (h + 1) * D)
        fkey = jnp.concatenate([f[:, 0, :, hs].reshape(-1, D) for f in (u0, u1)], axis=0)
        fval = ones_beside(jnp.concatenate([f[:, 1, :, hs].reshape(-1, D) for f in (u0, u1)], axis=0))
        for s, q in enumerate((q0, q1, q2, q3)):
            j = lax.rem(x - s + GROUPS, GROUPS)
            key = ks[pl.ds(j, 3), :, :, hs].reshape(keys, D)
            val = ones_beside(vs[pl.ds(j, 3), :, :, hs].reshape(keys, D))
            qq = q[:, :, hs].reshape(n, D)
            sc = scores(qq, key) + bias[s]
            sf = scores(qq, fkey)
            top = jnp.maximum(highest(sc), highest(sf))
            p = weigh(sc, top).astype(BF)
            pf = weigh(sf, top).astype(BF)
            r = mix(p, val) + mix(pf, fval)
            acc[s, :, hs] = r[:, :D]
            tops[s] = jnp.where(lane == h, top, tops[s])
            sums[s] = jnp.where(lane == h, r[:, D:], sums[s])
    for s in range(GROUPS):
        mo[s] = tops[s]
        lo[s] = sums[s]


def far_kernel(slots, xi, *refs):
    k = len(slots)
    qs, (acc, mi, li, t1, t2, bias), fars, outs = refs[:k], refs[k:k + 6], refs[k + 6:-k], refs[-k:]
    frames, width = qs[0].shape[:2]
    n = frames * width
    for h in range(GH):
        hs = slice(h * D, (h + 1) * D)
        key = jnp.concatenate([f[:, 0, :, hs].reshape(-1, D) for f in fars], axis=0)
        val = ones_beside(jnp.concatenate([f[:, 1, :, hs].reshape(-1, D) for f in fars], axis=0))
        qq = jnp.concatenate([q[:, :, hs].reshape(n, D) for q in qs], axis=0)
        sc = scores(qq, key)
        parts, evals = [], []
        for i, s in enumerate(slots):
            j = lax.rem(xi[0] - s + GROUPS, GROUPS)
            ekey = jnp.concatenate([t[pl.ds(j, 3), 0, :, hs].reshape(-1, D) for t in (t1, t2)], axis=0)
            evals.append(ones_beside(jnp.concatenate([t[pl.ds(j, 3), 1, :, hs].reshape(-1, D) for t in (t1, t2)], axis=0)))
            parts.append(scores(qq[i * n:(i + 1) * n], ekey) + bias[s])
        se = jnp.concatenate(parts, axis=0)
        mn = jnp.concatenate([mi[s, :, h:h + 1] for s in slots], axis=0)
        top = jnp.maximum(mn, jnp.maximum(highest(sc), highest(se)))
        p = weigh(sc, top).astype(BF)
        pe = weigh(se, top).astype(BF)
        fix = weigh(mn, top)
        r = mix(p, val)
        for i, (s, o) in enumerate(zip(slots, outs)):
            rs = slice(i * n, (i + 1) * n)
            both = r[rs] + mix(pe[rs], evals[i])
            tot = li[s, :, h:h + 1] * fix[rs] + both[:, D:]
            num = acc[s, :, hs] * fix[rs] + both[:, :D]
            o[:, :, hs] = (num / tot).astype(BF).reshape(frames, width, D)


def join_kernel(xi, r0, r1, r2, r3, out):
    for s, r in enumerate((r0, r1, r2, r3)):
        base = lax.rem(xi[0] + s, GROUPS) * GC
        out[:, 0, :, pl.ds(pl.multiple_of(base, D), GC)] = r[...]


def call(kernel, args, outs, smem=0, hbm=0, scratch=(), flops=1000000):
    specs = [pl.BlockSpec(memory_space=pltpu.SMEM)] * smem
    specs += [pl.BlockSpec(memory_space=pltpu.HBM)] * hbm
    specs += [pl.BlockSpec(memory_space=pltpu.VMEM)] * (len(args) - smem - hbm)
    many = isinstance(outs, (list, tuple))
    ospec = [pl.BlockSpec(memory_space=pltpu.VMEM) for _ in outs] if many else pl.BlockSpec(memory_space=pltpu.VMEM)
    size = sum(a.size * a.dtype.itemsize for a in args)
    return pl.pallas_call(
        kernel,
        out_shape=outs,
        in_specs=specs,
        out_specs=ospec,
        scratch_shapes=list(scratch),
        cost_estimate=pl.CostEstimate(flops=flops, bytes_accessed=size, transcendentals=0),
        compiler_params=pltpu.CompilerParams(vmem_limit_bytes=48 * 1024 * 1024),
    )(*args)


def xshift(s):
    return [(i, i // 4 * 4 + (i + s) % 4) for i in range(32)]


def yshift(s):
    return [(i, i // 16 * 16 + ((i // 4 + s) % 4) * 4 + i % 4) for i in range(32)]


def pairs(count, skip, width):
    out = []
    for b in range(skip, count - 1, 2):
        for i in range(width):
            out += [(b * width + i, (b + 1) * width + i), ((b + 1) * width + i, b * width + i)]
    return out


def per_device(queries, keys, values, window_mask, pos_t, pos_h, pos_w):
    frames, _, width, _ = queries.shape
    ti = lax.axis_index("tm")
    hi = lax.axis_index("height")
    x = hi % 4
    par = hi // 4 % 2
    xi = x.reshape(1).astype(jnp.int32)
    ri = par.reshape(1).astype(jnp.int32)
    fi = (ti % 2).reshape(1).astype(jnp.int32)
    both = ("tm", "height")
    sds = jax.ShapeDtypeStruct
    n = frames * width

    kvs = [sds((frames, 2, width, GC), BF)] * 4
    tab = sds((frames, width, D), F32)
    dma = pltpu.SemaphoreType.DMA
    *kv, far, cos_t, sin_t = call(
        kv_kernel, (xi, pos_h, *[pltpu.with_memory_space_constraint(a, pltpu.HBM) for a in (pos_t, pos_w, keys, values)]),
        kvs + [sds((4, 2, width, GC), BF), tab, tab], smem=2, hbm=4,
        scratch=(pltpu.SMEM((frames,), jnp.int32), pltpu.SMEM((width,), jnp.int32),
                 pltpu.VMEM((frames, width, HEADS * D), BF), pltpu.VMEM((frames, width, HEADS * D), BF),
                 dma((2,)), dma((frames,)), dma((frames,))))

    kvr = [kv[0]] + [lax.ppermute(kv[s], "height", xshift(s)) for s in (1, 2, 3)]

    twin = lax.ppermute(far, "tm", [(0, 1)])
    seed = jnp.where(ti == 1, twin, far)
    near = lambda k: [(r, 2 * k * 32 + r) for r in range(32)] if k < 4 else []
    cross = lambda k: [(32 + r, (2 * k + 1) * 32 + (r + 16) % 32) for r in range(32)]
    spread = [lax.ppermute(seed, both, near(3 - k) + cross(k)) if k < 3 else lax.ppermute(seed, both, cross(3))
              for k in range(4)]
    mine = jnp.where(ti == 0, far, (spread[0] + spread[1]) + (spread[2] + spread[3]))

    q = call(q_kernel, (xi, cos_t, sin_t, queries), [sds((frames, width, GC), BF)] * 4, smem=1)

    small = jnp.pad(window_mask.reshape(frames * 4, 27).astype(BF), ((0, 0), (0, D - 27)))
    masks = [small] + [lax.ppermute(small, "height", xshift(s)) for s in (1, 2, 3)]
    inner, outer = call(bias_kernel, (fi, *masks),
                        [sds((4, n, 3 * frames * width), F32), sds((4, n, 6 * width), F32)], smem=1)

    def row_of(j):
        at = (x - j) % 4
        return jnp.where(at < 2, jnp.where(at == 0, kvr[0], kvr[1]), jnp.where(at == 2, kvr[2], kvr[3]))

    h2 = lax.ppermute(row_of(3 * par), "height", pairs(8, 1, 4))
    h1 = lax.ppermute(row_of(3 - 3 * par), "height", pairs(8, 0, 4))
    rows = kvr + [h1, h2]
    edge = sds((len(rows), 2, width, GC), BF)
    inside, across = call(edge_kernel, (xi, ri, fi, *rows), [edge, edge], smem=3)
    t2 = lax.ppermute(across, "tm", pairs(8, 1, 1))
    t1 = lax.ppermute(inside, "tm", pairs(8, 0, 1))

    qr = [q[0]] + [lax.ppermute(q[s], "height", xshift(s)) for s in (1, 2, 3)]

    xf = [mine[0]] + [lax.ppermute(mine[s], "height", xshift(s)) for s in (1, 2, 3)]
    unit = jnp.stack(xf)
    units = [unit] + [lax.ppermute(unit, "height", yshift(s)) for s in (1, 3, 2)]
    swap = [(i, i ^ 1) for i in range(8)]
    units = units + [lax.ppermute(u, "tm", swap) for u in units]

    ext = pltpu.VMEM((GROUPS + 2, frames, width, GC), BF)
    acc, mo, lo = call(
        near_kernel, (xi, ri, *kvr, h1, h2, units[0], units[4], *qr, inner),
        [sds((4, n, GC), F32), sds((4, n, D), F32), sds((4, n, D), F32)],
        smem=2, scratch=(ext, ext))
    back = [None] * 4
    rest = units[1:4] + units[5:8]
    for slots in ((2,), (1, 3), (0,)):
        outs = call(functools.partial(far_kernel, slots),
                    (xi, *[qr[s] for s in slots], acc, mo, lo, t1, t2, outer, *rest),
                    [sds((frames, width, GC), BF)] * len(slots), smem=1)
        for s, o in zip(slots, outs):
            back[s] = lax.ppermute(o, "height", xshift(-s)) if s else o
    return call(join_kernel, (xi, *back), sds((frames, 1, width, HEADS * D), BF), smem=1)


def solution(mesh):
    wide = P("tm", "height", None, None)

    return jax.shard_map(
        per_device,
        mesh=mesh,
        in_specs=(wide, wide, wide, wide, P("tm"), P("height"), P()),
        out_specs=wide,
        check_vma=False,
    )
```
